128 devices in a mesh: req: 4 (over y), seq: 32 (over x, z, core).
Axes of the slice: x: 4, y: 4, z: 4, core: 2. Of those that a mesh axis runs over, the one named last changes fastest.
Arguments:
- query: bfloat16 [8, 2048, 2048], P('req', 'seq')
- fresh_kv: bfloat16 [8, 2048, 2048], P('req', 'seq'), may hold values from -6 to 6
- residual: bfloat16 [8, 2048, 2304], P('req', 'seq')
- kv_cache: bfloat16 [8, 64, 16, 2048], P('req', 'seq'), may hold values from -6 to 6
- page_table: int32 [8, 32, 2], P('req', 'seq'), may hold values from 0 to 1, each once within a row
- cache_length: int32 [8], replicated, may hold values from 256 to 1024, as said below
- slot_request: int32 [8], replicated, may hold values from 0 to 7, each once
- w_out: bfloat16 [2048, 2304], P('req'), may hold values from -0.125 to 0.125
- w_gate: bfloat16 [2304, 4608], P(None, 'req'), may hold values from -0.125 to 0.125
- w_up: bfloat16 [2304, 4608], P(None, 'req'), may hold values from -0.125 to 0.125
- w_down: bfloat16 [4608, 2304], P('req'), may hold values from -0.09375 to 0.09375
- gain_attn: float32 [2304], replicated, may hold values from 0.1 to 1.9
- gain_pre: float32 [2304], replicated, may hold values from 0.1 to 1.9
- gain_post: float32 [2304], replicated, may hold values from 0.1 to 1.9
Outputs:
- output: bfloat16 [8, 2048, 2304], P('req', 'seq')
The draws below stay inside these ranges and needn't reach their ends.
Inputs may be any that keep to these rules, and one draw needn't show every extreme that they name: `slot_request`: each request has exactly one slot. `page_table`: each row of 2 entries names each of 0 to 1 once. `cache_length`: some request has exactly 1024 cached positions and some exactly 256.
All inputs are finite; a program needn't handle non-finite values.
Results may differ from the reference program's by a relative error of at most 0.015.
Values may be sent and summed in bfloat16 or wider, within the bound.
A program may use at most 192 MiB of HBM per device.

```python
import math
import jax
import jax.numpy as jnp
from jax import lax

D = 2304
H = 8
KV = 4
HD = 256
FF = 4608
PAGE = 16
PAGES_DEV = 2
REQS = 8
C = 2048
NPAGE = 64
L_MAX = 1024
N_SEQ = 32


def draw_query(key, part):
    base = jnp.clip(jax.random.normal(jax.random.fold_in(key, 11), (REQS, C, H * HD), jnp.float32), -6.0, 6.0)
    return base.astype(jnp.bfloat16)


def draw_residual(key, part):
    base = jnp.clip(jax.random.normal(jax.random.fold_in(key, 21), (REQS, C, D), jnp.float32), -6.0, 6.0)
    return base.astype(jnp.bfloat16)


def draw_cache_length(key, part):
    lengths = jax.random.randint(jax.random.fold_in(key, 31), (REQS,), L_MAX // 4, L_MAX + 1)
    order = jax.random.permutation(jax.random.fold_in(key, 32), REQS)
    lengths = lengths.at[order[0]].set(L_MAX)
    lengths = lengths.at[order[1]].set(L_MAX // 4)
    return lengths.astype(jnp.int32)


def block_scale(own_key, extent, pieces, smallest, largest):
    level = 1.0
    for dim, parts in pieces:
        steps = jax.random.uniform(jax.random.fold_in(jax.random.fold_in(own_key, 6), dim), (parts,), jnp.float32, smallest / len(pieces), largest / len(pieces))
        level = level * jnp.repeat(jnp.exp(steps), extent[dim] // parts).reshape((-1,) + (1,) * (len(extent) - 1 - dim))
    return level


def bell_draw(key, extent, width, bound, cuts=(), kind=jnp.bfloat16):
    drawn = width * jax.random.normal(key, extent, jnp.float32)
    if cuts:
        drawn = drawn * block_scale(key, extent, cuts, -0.22, 0.18)
    return jnp.clip(drawn, -bound, bound).astype(kind)


def setup_inputs(seed: int = 0) -> dict:
    splits = jax.random.split(jax.random.key(seed), 15)
    query = draw_query(jax.random.fold_in(splits[14], 71), 0)
    fresh_kv = bell_draw(splits[1], (REQS, C, 2 * KV * HD), 1.0, 6.0, ((0, 4), (1, 32)))
    residual = draw_residual(jax.random.fold_in(splits[14], 71), 0)
    kv_cache = bell_draw(splits[3], (REQS, NPAGE, PAGE, 2 * KV * HD), 1.0, 6.0, ((0, 4), (1, 32)))
    page_table = jax.vmap(lambda own: jax.random.permutation(own, PAGES_DEV))(jax.random.split(splits[4], REQS * N_SEQ)).reshape((REQS, N_SEQ, PAGES_DEV)).astype(jnp.int32)
    cache_length = draw_cache_length(jax.random.fold_in(splits[14], 71), 0)
    slot_request = jax.random.permutation(splits[6], REQS).astype(jnp.int32)
    w_out = bell_draw(splits[7], (H * HD, D), (H * HD) ** -0.5, 0.125, ((0, 4),))
    w_gate = bell_draw(splits[8], (D, FF), D ** -0.5, 0.125, ((1, 4),))
    w_up = bell_draw(splits[9], (D, FF), D ** -0.5, 0.125, ((1, 4),))
    w_down = bell_draw(splits[10], (FF, D), FF ** -0.5, 0.09375, ((0, 4),))
    gain_attn = jnp.clip(1.0 + 0.18 * jax.random.normal(splits[11], (D,), jnp.float32), 0.1, 1.9)
    gain_pre = jnp.clip(1.0 + 0.18 * jax.random.normal(splits[12], (D,), jnp.float32), 0.1, 1.9)
    gain_post = jnp.clip(1.0 + 0.18 * jax.random.normal(splits[13], (D,), jnp.float32), 0.1, 1.9)
    return {"query": query, "fresh_kv": fresh_kv, "residual": residual, "kv_cache": kv_cache, "page_table": page_table, "cache_length": cache_length, "slot_request": slot_request, "w_out": w_out, "w_gate": w_gate, "w_up": w_up, "w_down": w_down, "gain_attn": gain_attn, "gain_pre": gain_pre, "gain_post": gain_post}


SOFT_CAP = 50.0
EPSILON = 1e-06

def rms_scale(tensor, scale_gain):
    return tensor * lax.rsqrt(lax.optimization_barrier(jnp.mean(tensor * tensor, axis=-1, keepdims=True)) + EPSILON) * scale_gain

def attend(queries, stacked, allowed):
    row_count = queries.shape[0]
    group_size = H // KV
    kv_width = KV * HD
    grouped = queries.reshape(row_count, KV, group_size, HD).astype(jnp.float32)
    key_rows = stacked[:, :kv_width].reshape(-1, KV, HD).astype(jnp.float32)
    value_rows = stacked[:, kv_width:].reshape(-1, KV, HD).astype(jnp.float32)
    scores = jnp.einsum('nkgd,mkd->kgnm', grouped, key_rows) * HD ** (-0.5)
    capped = SOFT_CAP * jnp.tanh(scores / SOFT_CAP)
    rounded = lax.optimization_barrier(jnp.where(allowed[None, None], jnp.exp(capped), 0.0).astype(jnp.bfloat16))
    weights = rounded.astype(jnp.float32)
    denominator = lax.optimization_barrier(jnp.sum(weights, axis=-1))
    summed = jnp.einsum('kgnm,mkd->nkgd', weights, value_rows)
    attended = summed / jnp.transpose(denominator, (2, 0, 1))[..., None]
    return attended.reshape(row_count, H * HD).astype(jnp.bfloat16)

def reference(query, fresh_kv, residual, kv_cache, page_table, cache_length, slot_request, w_out, w_gate, w_up, w_down, gain_attn, gain_pre, gain_post):
    pair_width = 2 * KV * HD
    paged = kv_cache.reshape(REQS, N_SEQ, PAGES_DEV, PAGE, pair_width)
    req_index = jnp.arange(REQS)[:, None, None]
    block_index = jnp.arange(N_SEQ)[None, :, None]
    ordered = paged[req_index, block_index, page_table].reshape(REQS, L_MAX, pair_width)
    block_len = math.gcd(C, 512)

    def one_slot(slot_data):
        queries, fresh_rows, residual_rows, request = slot_data
        cache_rows = ordered[request]
        length = cache_length[request]
        stacked = jnp.concatenate([cache_rows, fresh_rows], axis=0)
        cache_live = jnp.arange(L_MAX) < length

        def one_block(first):
            row_ids = first + jnp.arange(block_len)
            query_block = lax.dynamic_slice_in_dim(queries, first, block_len, 0)
            fresh_live = jnp.arange(C)[None, :] <= row_ids[:, None]
            allowed = jnp.concatenate([jnp.broadcast_to(cache_live[None, :], (block_len, L_MAX)), fresh_live], axis=1)
            return attend(query_block, stacked, allowed)
        starts = (jnp.arange(C // block_len) * block_len).astype(jnp.int32)
        attended = lax.map(one_block, starts).reshape(C, H * HD)
        mixed = jnp.dot(attended, w_out, preferred_element_type=jnp.float32)
        layer_state = residual_rows.astype(jnp.float32) + rms_scale(mixed, gain_attn)
        normed = rms_scale(layer_state, gain_pre).astype(jnp.bfloat16)
        gate_proj = jnp.dot(normed, w_gate, preferred_element_type=jnp.float32)
        up_proj = jnp.dot(normed, w_up, preferred_element_type=jnp.float32)
        hidden = (jax.nn.gelu(gate_proj, approximate=True) * up_proj).astype(jnp.bfloat16)
        down_proj = jnp.dot(hidden, w_down, preferred_element_type=jnp.float32)
        return (layer_state + rms_scale(down_proj, gain_post)).astype(jnp.bfloat16)
    return lax.map(one_slot, (query, fresh_kv, residual, slot_request))
```

```python
import jax
import jax.numpy as jnp
from jax import lax
from jax.experimental import pallas as pl
from jax.experimental.pallas import tpu as pltpu
from jax.sharding import PartitionSpec as P

H = 8
KV = 4
HD = 256
SOFT_CAP = 50.0
EPSILON = 1e-06
LOG2E = 1.4426950408889634
MESH = pl.DeviceIdType.MESH


def rms_scale(tensor, scale_gain):
    return (
        tensor * lax.rsqrt(jnp.mean(tensor * tensor, axis=-1, keepdims=True) + EPSILON) * scale_gain
    )


def attention_kernel(
    slot_ref,
    len_ref,
    q_ref,
    f_ref,
    c_ref,
    att_ref,
    qbuf,
    kvf,
    kvc,
    stage,
    order,
    obuf,
    acc,
    den,
    ca_send,
    ca_recv,
    q_send,
    q_recv,
    f_send,
    f_recv,
    cb_send,
    c_recv,
    fw_send,
    fd_recv,
    r_send,
    r_recv,
):
    y = lax.axis_index("req")
    s = lax.axis_index("seq")
    core = s % 2
    half = (s // 2) % 2
    slot = s // 4
    quarter = s % 4
    sibling = s + 1 - 2 * core

    def remote(src, dst, send, recv, to):
        return pltpu.make_async_remote_copy(
            src_ref=src, dst_ref=dst, send_sem=send, recv_sem=recv, device_id=to, device_id_type=MESH
        )

    def lanes(start):
        return pl.ds(pl.multiple_of(start, 256), 256)

    def cache_part(k, h):
        return c_ref.at[:, :, lanes(h * 1024 + k * 256)]

    def stage_part(owner, h):
        return stage.at[pl.ds(2 * owner, 2), :, pl.ds(h * 256, 256)]

    for d in range(1, 4):
        k = (y + d) % 4
        for h in range(2):
            remote(
                cache_part(k, h), stage_part(y, h), ca_send.at[d, h], ca_recv.at[y, h], (k, s)
            ).start()
    for h in range(2):
        pltpu.make_async_copy(cache_part(y, h), stage_part(y, h), ca_recv.at[y, h]).start()

    def fresh_copies(k, j, p, act):
        target = 4 * (2 * y + j) + 2 * p + core
        own = (k == y) & (target == s)
        n = (k * 2 + j) * 2 + p
        for h in range(2):
            src = f_ref.at[j, :, lanes(h * 1024 + k * 256)]
            dst = kvf.at[s, :, pl.ds(h * 256, 256)]

            @pl.when(jnp.logical_not(own))
            def _():
                cp = remote(src, dst, f_send.at[n, h], fd_recv.at[s, h], (k, target))
                if act == "start":
                    cp.start()
                else:
                    cp.wait_send()

            if act == "start":

                @pl.when(own)
                def _():
                    pltpu.make_async_copy(src, dst, fd_recv.at[s, h]).start()

    def query_copies(k, j, act):
        target = 4 * (2 * y + j) + quarter
        own = (k == y) & (target == s)
        n = k * 2 + j
        src = q_ref.at[j, :, pl.ds(pl.multiple_of(k * 512, 512), 512)]
        dst = qbuf.at[s // 4]

        @pl.when(jnp.logical_not(own))
        def _():
            cp = remote(src, dst, q_send.at[n], q_recv.at[s // 4], (k, target))
            if act == "start":
                cp.start()
            else:
                cp.wait_send()

        if act == "start":

            @pl.when(own)
            def _():
                pltpu.make_async_copy(src, dst, q_recv.at[s // 4]).start()

    def new_rows(act):
        for d in range(4):
            k = (y + d) % 4
            for j in range(2):
                for p in range(2):
                    fresh_copies(k, j, p, act)
        for d in range(4):
            k = (y + d) % 4
            for j in range(2):
                query_copies(k, j, act)

    new_rows("start")

    for owner in range(4):
        for h in range(2):
            pltpu.make_async_copy(stage_part(owner, h), stage_part(owner, h), ca_recv.at[owner, h]).wait()
    for i in range(8):
        order[i] = stage[slot_ref[i]]

    def cache_copies(i, p, act):
        target = 4 * i + 2 * p + core
        own = target == s
        src = order.at[i]
        dst = kvc.at[s]

        @pl.when(jnp.logical_not(own))
        def _():
            cp = remote(src, dst, cb_send.at[i, p], c_recv.at[s], (y, target))
            if act == "start":
                cp.start()
            else:
                cp.wait_send()

        if act == "start":

            @pl.when(own)
            def _():
                pltpu.make_async_copy(src, dst, c_recv.at[s]).start()

    for i in range(8):
        for p in range(2):
            cache_copies(i, p, "start")

    for j in range(16):
        src = 2 * j + core
        for h in range(2):
            part = kvf.at[src, :, pl.ds(h * 256, 256)]
            pltpu.make_async_copy(part, part, fd_recv.at[src, h]).wait()
        remote(kvf.at[src], kvf.at[src], fw_send.at[j, 0], f_recv.at[j], (y, sibling)).start()
    for j in range(16):
        src = 2 * j + core
        pltpu.make_async_copy(kvc.at[src], kvc.at[src], c_recv.at[src]).wait()
        remote(kvc.at[src], kvc.at[src], fw_send.at[j, 1], c_recv.at[src], (y, sibling)).start()
    for j in range(8):
        pltpu.make_async_copy(qbuf.at[j], qbuf.at[j], q_recv.at[j]).wait()
    for j in range(16):
        src = 2 * j + 1 - core
        pltpu.make_async_copy(kvf.at[src], kvf.at[src], f_recv.at[j]).wait()
        pltpu.make_async_copy(kvc.at[src], kvc.at[src], c_recv.at[src]).wait()

    length = len_ref[0]
    for n in range(12):
        fresh = n - 4
        if n < 4:
            keys = kvc[8 * n : 8 * n + 8].reshape(256, 512)
            first = 0
        else:
            keys = kvf[4 * fresh : 4 * fresh + 4].reshape(256, 512)
            first = fresh
        rows = 512 - 64 * first
        for g in range(2):
            queries = qbuf[first:, :, g * 256 : (g + 1) * 256].reshape(rows, 256)
            scores = lax.dot_general(
                queries, keys[:, :256], (((1,), (1,)), ((), ())), preferred_element_type=jnp.float32
            )
            weights = jnp.exp2(
                jnp.tanh(scores * (HD**-0.5 / SOFT_CAP)) * (SOFT_CAP * LOG2E)
            )
            if 0 < n < 4:
                lane = lax.broadcasted_iota(jnp.int32, (rows, 256), 1)
                weights = jnp.where(lane + 256 * n < length, weights, 0.0)
            if n >= 4:
                lane = lax.broadcasted_iota(jnp.int32, (64, 256), 1)
                line = lax.broadcasted_iota(jnp.int32, (64, 256), 0)
                edge = jnp.where(lane <= quarter * 64 + line, weights[:64], 0.0)
                weights = jnp.concatenate([edge, weights[64:]], axis=0) if rows > 64 else edge
            rounded = weights.astype(jnp.bfloat16)
            wide = rounded.astype(jnp.float32)
            total = wide[:, :128] + wide[:, 128:]
            summed = jnp.dot(rounded, keys[:, 256:], preferred_element_type=jnp.float32)
            if n == 0:
                acc[g] = summed
                den[g] = total
            else:
                acc[g, 64 * first :, :] += summed
                den[g, 64 * first :, :] += total
    for g in range(2):
        bottom = jnp.sum(den[g], axis=-1, keepdims=True)
        obuf[:, :, g * 256 : (g + 1) * 256] = (
            (acc[g] / bottom).astype(jnp.bfloat16).reshape(8, 64, 256)
        )

    def result_copies(j, act):
        target = quarter + 4 * j
        own = target == s
        src = obuf.at[j]
        dst = att_ref.at[slot]

        @pl.when(jnp.logical_not(own))
        def _():
            cp = remote(src, dst, r_send.at[j], r_recv.at[slot], (y, target))
            if act == "start":
                cp.start()
            else:
                cp.wait_send()

        if act == "start":

            @pl.when(own)
            def _():
                pltpu.make_async_copy(src, dst, r_recv.at[slot]).start()

    for j in range(8):
        result_copies(j, "start")
    for i in range(8):
        pltpu.make_async_copy(att_ref.at[i], att_ref.at[i], r_recv.at[i]).wait()

    for d in range(1, 4):
        k = (y + d) % 4
        for h in range(2):
            remote(
                cache_part(k, h), stage_part(y, h), ca_send.at[d, h], ca_recv.at[y, h], (k, s)
            ).wait_send()
    new_rows("wait")
    for i in range(8):
        for p in range(2):
            cache_copies(i, p, "wait")
    for j in range(16):
        src = 2 * j + core
        remote(kvf.at[src], kvf.at[src], fw_send.at[j, 0], f_recv.at[j], (y, sibling)).wait_send()
        remote(kvc.at[src], kvc.at[src], fw_send.at[j, 1], c_recv.at[src], (y, sibling)).wait_send()
    for j in range(8):
        result_copies(j, "wait")


def attention(slot_request, length, query, fresh, cache):
    dma = pltpu.SemaphoreType.DMA
    return pl.pallas_call(
        attention_kernel,
        out_shape=jax.ShapeDtypeStruct((8, 64, 512), jnp.bfloat16),
        in_specs=[
            pl.BlockSpec(memory_space=pltpu.SMEM),
            pl.BlockSpec(memory_space=pltpu.SMEM),
            pl.BlockSpec(memory_space=pltpu.VMEM),
            pl.BlockSpec(memory_space=pltpu.VMEM),
            pl.BlockSpec(memory_space=pltpu.VMEM),
        ],
        out_specs=pl.BlockSpec(memory_space=pltpu.VMEM),
        scratch_shapes=[
            pltpu.VMEM((8, 64, 512), jnp.bfloat16),
            pltpu.VMEM((32, 64, 512), jnp.bfloat16),
            pltpu.VMEM((32, 32, 512), jnp.bfloat16),
            pltpu.VMEM((8, 32, 512), jnp.bfloat16),
            pltpu.VMEM((8, 32, 512), jnp.bfloat16),
            pltpu.VMEM((8, 64, 512), jnp.bfloat16),
            pltpu.VMEM((2, 512, 256), jnp.float32),
            pltpu.VMEM((2, 512, 128), jnp.float32),
            dma((4, 2)),
            dma((4, 2)),
            dma((8,)),
            dma((8,)),
            dma((16, 2)),
            dma((16,)),
            dma((8, 2)),
            dma((32,)),
            dma((16, 2)),
            dma((32, 2)),
            dma((8,)),
            dma((8,)),
        ],
        compiler_params=pltpu.CompilerParams(
            has_side_effects=True, vmem_limit_bytes=40 * 1024 * 1024
        ),
        name="attention",
    )(slot_request, length, query, fresh, cache)


def body(
    query,
    fresh_kv,
    residual,
    kv_cache,
    page_table,
    cache_length,
    slot_request,
    w_out,
    w_gate,
    w_up,
    w_down,
    gain_attn,
    gain_pre,
    gain_post,
):
    req_dev, row_count = (query.shape[0], query.shape[1])
    pages_dev, page_len, pair_width = kv_cache.shape[1:]
    my_seq = lax.axis_index("seq")
    ordered = jnp.where(
        (page_table[:, 0, :] == 1)[:, :, None, None], kv_cache[:, 1:2], kv_cache[:, 0:1]
    ).reshape(req_dev, pages_dev * page_len, pair_width)
    my_request = lax.dynamic_slice_in_dim(slot_request, my_seq // 4, 1)
    my_len = jnp.sum(
        jnp.where(my_request == jnp.arange(cache_length.shape[0]), cache_length, 0)
    ).reshape(1)
    attended = attention(slot_request, my_len, query, fresh_kv, ordered)
    partial_out = jnp.einsum("srk,kd->srd", attended, w_out, preferred_element_type=jnp.float32)
    mixed = lax.psum_scatter(
        partial_out.astype(jnp.bfloat16), "req", scatter_dimension=0, tiled=True
    ).astype(jnp.float32)
    layer_state = residual.astype(jnp.float32) + rms_scale(mixed, gain_attn)
    normed = rms_scale(layer_state, gain_pre).astype(jnp.bfloat16)
    portion = lax.all_gather(normed, "req", axis=0, tiled=True)
    gate_proj = jnp.einsum("srd,df->srf", portion, w_gate, preferred_element_type=jnp.float32)
    up_proj = jnp.einsum("srd,df->srf", portion, w_up, preferred_element_type=jnp.float32)
    hidden = (jax.nn.gelu(gate_proj, approximate=True) * up_proj).astype(jnp.bfloat16)
    mlp_out = lax.psum_scatter(
        jnp.einsum("srf,fd->srd", hidden, w_down, preferred_element_type=jnp.float32).astype(
            jnp.bfloat16
        ),
        "req",
        scatter_dimension=0,
        tiled=True,
    ).astype(jnp.float32)
    return (layer_state + rms_scale(mlp_out, gain_post)).astype(jnp.bfloat16)


def solution(mesh):
    in_specs = (
        P("req", "seq", None),
        P("req", "seq", None),
        P("req", "seq", None),
        P("req", "seq", None, None),
        P("req", "seq", None),
        P(),
        P(),
        P("req", None),
        P(None, "req"),
        P(None, "req"),
        P("req", None),
        P(),
        P(),
        P(),
    )
    out_specs = P("req", "seq", None)
    return jax.shard_map(body, mesh=mesh, in_specs=in_specs, out_specs=out_specs, check_vma=False)
```

```python
import jax
import jax.numpy as jnp
from jax import lax
from jax.experimental import pallas as pl
from jax.experimental.pallas import tpu as pltpu
from jax.sharding import PartitionSpec as P

H = 8
KV = 4
HD = 256
SOFT_CAP = 50.0
EPSILON = 1e-06
LOG2E = 1.4426950408889634
MESH = pl.DeviceIdType.MESH


def rms_scale(tensor, scale_gain):
    return (
        tensor * lax.rsqrt(jnp.mean(tensor * tensor, axis=-1, keepdims=True) + EPSILON) * scale_gain
    )


def role(s):
    x, z = s // 8, (s // 2) % 4
    return 2 * ((x + z) % 4) + x % 2, 2 * (x // 2) + s % 2


def device_of(slot, quarter):
    x = 2 * (quarter // 2) + slot % 2
    z = (slot // 2 - x + 4) % 4
    return 8 * x + 2 * z + quarter % 2


def attention_kernel(
    slot_ref,
    len_ref,
    q_ref,
    f_ref,
    c_ref,
    att_ref,
    qbuf,
    kvf,
    kvc,
    stage,
    order,
    obuf,
    acc,
    den,
    ca_send,
    ca_recv,
    q_send,
    q_recv,
    f_send,
    f_recv,
    cb_send,
    c_recv,
    fw_send,
    fd_recv,
    r_send,
    r_recv,
):
    y = lax.axis_index("req")
    s = lax.axis_index("seq")
    core = s % 2
    slot, quarter = role(s)
    sibling = s + 1 - 2 * core

    def remote(src, dst, send, recv, to):
        return pltpu.make_async_remote_copy(
            src_ref=src, dst_ref=dst, send_sem=send, recv_sem=recv, device_id=to, device_id_type=MESH
        )

    def lanes(start):
        return pl.ds(pl.multiple_of(start, 256), 256)

    def cache_part(k, h):
        return c_ref.at[:, :, lanes(h * 1024 + k * 256)]

    def stage_part(owner, h):
        return stage.at[pl.ds(2 * owner, 2), :, pl.ds(h * 256, 256)]

    for d in range(1, 4):
        k = (y + d) % 4
        for h in range(2):
            remote(
                cache_part(k, h), stage_part(y, h), ca_send.at[d, h], ca_recv.at[y, h], (k, s)
            ).start()
    for h in range(2):
        pltpu.make_async_copy(cache_part(y, h), stage_part(y, h), ca_recv.at[y, h]).start()

    def fresh_copies(k, j, p, act):
        target = device_of(2 * y + j, 2 * p + core)
        own = (k == y) & (target == s)
        n = (k * 2 + j) * 2 + p
        for h in range(2):
            src = f_ref.at[j, :, lanes(h * 1024 + k * 256)]
            dst = kvf.at[s, :, pl.ds(h * 256, 256)]

            @pl.when(jnp.logical_not(own))
            def _():
                cp = remote(src, dst, f_send.at[n, h], fd_recv.at[s, h], (k, target))
                if act == "start":
                    cp.start()
                else:
                    cp.wait_send()

            if act == "start":

                @pl.when(own)
                def _():
                    pltpu.make_async_copy(src, dst, fd_recv.at[s, h]).start()

    def query_copies(k, j, act):
        target = device_of(2 * y + j, s % 4)
        own = (k == y) & (target == s)
        n = k * 2 + j
        src = q_ref.at[j, :, pl.ds(pl.multiple_of(k * 512, 512), 512)]
        dst = qbuf.at[s // 4]

        @pl.when(jnp.logical_not(own))
        def _():
            cp = remote(src, dst, q_send.at[n], q_recv.at[s // 4], (k, target))
            if act == "start":
                cp.start()
            else:
                cp.wait_send()

        if act == "start":

            @pl.when(own)
            def _():
                pltpu.make_async_copy(src, dst, q_recv.at[s // 4]).start()

    def new_rows(act):
        for d in range(4):
            k = (y + d) % 4
            for j in range(2):
                for p in range(2):
                    fresh_copies(k, j, p, act)
        for d in range(4):
            k = (y + d) % 4
            for j in range(2):
                query_copies(k, j, act)

    new_rows("start")

    for owner in range(4):
        for h in range(2):
            pltpu.make_async_copy(stage_part(owner, h), stage_part(owner, h), ca_recv.at[owner, h]).wait()
    for i in range(8):
        order[i] = stage[slot_ref[i]]

    def cache_copies(i, p, act):
        target = device_of(i, 2 * p + core)
        own = target == s
        src = order.at[i]
        dst = kvc.at[s]

        @pl.when(jnp.logical_not(own))
        def _():
            cp = remote(src, dst, cb_send.at[i, p], c_recv.at[s], (y, target))
            if act == "start":
                cp.start()
            else:
                cp.wait_send()

        if act == "start":

            @pl.when(own)
            def _():
                pltpu.make_async_copy(src, dst, c_recv.at[s]).start()

    for i in range(8):
        for p in range(2):
            cache_copies(i, p, "start")

    for j in range(16):
        src = 2 * j + core
        for h in range(2):
            part = kvf.at[src, :, pl.ds(h * 256, 256)]
            pltpu.make_async_copy(part, part, fd_recv.at[src, h]).wait()
        remote(kvf.at[src], kvf.at[src], fw_send.at[j, 0], f_recv.at[j], (y, sibling)).start()
    for j in range(16):
        src = 2 * j + core
        pltpu.make_async_copy(kvc.at[src], kvc.at[src], c_recv.at[src]).wait()
        remote(kvc.at[src], kvc.at[src], fw_send.at[j, 1], c_recv.at[src], (y, sibling)).start()
    for j in range(8):
        pltpu.make_async_copy(qbuf.at[j], qbuf.at[j], q_recv.at[j]).wait()
    for j in range(16):
        src = 2 * j + 1 - core
        pltpu.make_async_copy(kvf.at[src], kvf.at[src], f_recv.at[j]).wait()
        pltpu.make_async_copy(kvc.at[src], kvc.at[src], c_recv.at[src]).wait()

    length = len_ref[0]
    for n in range(12):
        fresh = n - 4
        if n < 4:
            keys = kvc[8 * n : 8 * n + 8].reshape(256, 512)
            first = 0
        else:
            keys = kvf[4 * fresh : 4 * fresh + 4].reshape(256, 512)
            first = fresh
        rows = 512 - 64 * first
        for g in range(2):
            queries = qbuf[first:, :, g * 256 : (g + 1) * 256].reshape(rows, 256)
            scores = lax.dot_general(
                queries, keys[:, :256], (((1,), (1,)), ((), ())), preferred_element_type=jnp.float32
            )
            weights = jnp.exp2(
                jnp.tanh(scores * (HD**-0.5 / SOFT_CAP)) * (SOFT_CAP * LOG2E)
            )
            if 0 < n < 4:
                lane = lax.broadcasted_iota(jnp.int32, (rows, 256), 1)
                weights = jnp.where(lane + 256 * n < length, weights, 0.0)
            if n >= 4:
                lane = lax.broadcasted_iota(jnp.int32, (64, 256), 1)
                line = lax.broadcasted_iota(jnp.int32, (64, 256), 0)
                edge = jnp.where(lane <= quarter * 64 + line, weights[:64], 0.0)
                weights = jnp.concatenate([edge, weights[64:]], axis=0) if rows > 64 else edge
            rounded = weights.astype(jnp.bfloat16)
            wide = rounded.astype(jnp.float32)
            total = wide[:, :128] + wide[:, 128:]
            summed = jnp.dot(rounded, keys[:, 256:], preferred_element_type=jnp.float32)
            if n == 0:
                acc[g] = summed
                den[g] = total
            else:
                acc[g, 64 * first :, :] += summed
                den[g, 64 * first :, :] += total
    for g in range(2):
        bottom = jnp.sum(den[g], axis=-1, keepdims=True)
        obuf[:, :, g * 256 : (g + 1) * 256] = (
            (acc[g] / bottom).astype(jnp.bfloat16).reshape(8, 64, 256)
        )

    def result_copies(j, act):
        target = quarter + 4 * j
        own = target == s
        src = obuf.at[j]
        dst = att_ref.at[slot]

        @pl.when(jnp.logical_not(own))
        def _():
            cp = remote(src, dst, r_send.at[j], r_recv.at[slot], (y, target))
            if act == "start":
                cp.start()
            else:
                cp.wait_send()

        if act == "start":

            @pl.when(own)
            def _():
                pltpu.make_async_copy(src, dst, r_recv.at[slot]).start()

    for j in range(8):
        result_copies(j, "start")
    for i in range(8):
        pltpu.make_async_copy(att_ref.at[i], att_ref.at[i], r_recv.at[i]).wait()

    for d in range(1, 4):
        k = (y + d) % 4
        for h in range(2):
            remote(
                cache_part(k, h), stage_part(y, h), ca_send.at[d, h], ca_recv.at[y, h], (k, s)
            ).wait_send()
    new_rows("wait")
    for i in range(8):
        for p in range(2):
            cache_copies(i, p, "wait")
    for j in range(16):
        src = 2 * j + core
        remote(kvf.at[src], kvf.at[src], fw_send.at[j, 0], f_recv.at[j], (y, sibling)).wait_send()
        remote(kvc.at[src], kvc.at[src], fw_send.at[j, 1], c_recv.at[src], (y, sibling)).wait_send()
    for j in range(8):
        result_copies(j, "wait")


def attention(slot_request, length, query, fresh, cache):
    dma = pltpu.SemaphoreType.DMA
    return pl.pallas_call(
        attention_kernel,
        out_shape=jax.ShapeDtypeStruct((8, 64, 512), jnp.bfloat16),
        in_specs=[
            pl.BlockSpec(memory_space=pltpu.SMEM),
            pl.BlockSpec(memory_space=pltpu.SMEM),
            pl.BlockSpec(memory_space=pltpu.VMEM),
            pl.BlockSpec(memory_space=pltpu.VMEM),
            pl.BlockSpec(memory_space=pltpu.VMEM),
        ],
        out_specs=pl.BlockSpec(memory_space=pltpu.VMEM),
        scratch_shapes=[
            pltpu.VMEM((8, 64, 512), jnp.bfloat16),
            pltpu.VMEM((32, 64, 512), jnp.bfloat16),
            pltpu.VMEM((32, 32, 512), jnp.bfloat16),
            pltpu.VMEM((8, 32, 512), jnp.bfloat16),
            pltpu.VMEM((8, 32, 512), jnp.bfloat16),
            pltpu.VMEM((8, 64, 512), jnp.bfloat16),
            pltpu.VMEM((2, 512, 256), jnp.float32),
            pltpu.VMEM((2, 512, 128), jnp.float32),
            dma((4, 2)),
            dma((4, 2)),
            dma((8,)),
            dma((8,)),
            dma((16, 2)),
            dma((16,)),
            dma((8, 2)),
            dma((32,)),
            dma((16, 2)),
            dma((32, 2)),
            dma((8,)),
            dma((8,)),
        ],
        compiler_params=pltpu.CompilerParams(
            has_side_effects=True, vmem_limit_bytes=40 * 1024 * 1024
        ),
        name="attention",
    )(slot_request, length, query, fresh, cache)


def body(
    query,
    fresh_kv,
    residual,
    kv_cache,
    page_table,
    cache_length,
    slot_request,
    w_out,
    w_gate,
    w_up,
    w_down,
    gain_attn,
    gain_pre,
    gain_post,
):
    req_dev, row_count = (query.shape[0], query.shape[1])
    pages_dev, page_len, pair_width = kv_cache.shape[1:]
    my_seq = lax.axis_index("seq")
    ordered = jnp.where(
        (page_table[:, 0, :] == 1)[:, :, None, None], kv_cache[:, 1:2], kv_cache[:, 0:1]
    ).reshape(req_dev, pages_dev * page_len, pair_width)
    my_request = lax.dynamic_slice_in_dim(slot_request, role(my_seq)[0], 1)
    my_len = jnp.sum(
        jnp.where(my_request == jnp.arange(cache_length.shape[0]), cache_length, 0)
    ).reshape(1)
    attended = attention(slot_request, my_len, query, fresh_kv, ordered)
    partial_out = jnp.einsum("srk,kd->srd", attended, w_out, preferred_element_type=jnp.float32)
    mixed = lax.psum_scatter(
        partial_out.astype(jnp.bfloat16), "req", scatter_dimension=0, tiled=True
    ).astype(jnp.float32)
    layer_state = residual.astype(jnp.float32) + rms_scale(mixed, gain_attn)
    normed = rms_scale(layer_state, gain_pre).astype(jnp.bfloat16)
    portion = lax.all_gather(normed, "req", axis=0, tiled=True)
    gate_proj = jnp.einsum("srd,df->srf", portion, w_gate, preferred_element_type=jnp.float32)
    up_proj = jnp.einsum("srd,df->srf", portion, w_up, preferred_element_type=jnp.float32)
    hidden = (jax.nn.gelu(gate_proj, approximate=True) * up_proj).astype(jnp.bfloat16)
    mlp_out = lax.psum_scatter(
        jnp.einsum("srf,fd->srd", hidden, w_down, preferred_element_type=jnp.float32).astype(
            jnp.bfloat16
        ),
        "req",
        scatter_dimension=0,
        tiled=True,
    ).astype(jnp.float32)
    return (layer_state + rms_scale(mlp_out, gain_post)).astype(jnp.bfloat16)


def solution(mesh):
    in_specs = (
        P("req", "seq", None),
        P("req", "seq", None),
        P("req", "seq", None),
        P("req", "seq", None, None),
        P("req", "seq", None),
        P(),
        P(),
        P("req", None),
        P(None, "req"),
        P(None, "req"),
        P("req", None),
        P(),
        P(),
        P(),
    )
    out_specs = P("req", "seq", None)
    return jax.shard_map(body, mesh=mesh, in_specs=in_specs, out_specs=out_specs, check_vma=False)
```

```python
import jax
import jax.numpy as jnp
from jax import lax
from jax.experimental import pallas as pl
from jax.experimental.pallas import tpu as pltpu
from jax.sharding import PartitionSpec as P

H = 8
KV = 4
HD = 256
SOFT_CAP = 50.0
EPSILON = 1e-06
LOG2E = 1.4426950408889634
MESH = pl.DeviceIdType.MESH


def rms_scale(tensor, scale_gain):
    return (
        tensor * lax.rsqrt(jnp.mean(tensor * tensor, axis=-1, keepdims=True) + EPSILON) * scale_gain
    )


def role(s):
    x, z = s // 8, (s // 2) % 4
    return 2 * ((x + z) % 4) + x % 2, 2 * (x // 2) + s % 2


def device_of(slot, quarter):
    x = 2 * (quarter // 2) + slot % 2
    z = (slot // 2 - x + 4) % 4
    return 8 * x + 2 * z + quarter % 2


def attention_kernel(
    slot_ref,
    len_ref,
    q_ref,
    f_ref,
    c_ref,
    att_ref,
    qbuf,
    kvf,
    kvc,
    stage,
    order,
    obuf,
    acc,
    den,
    ca_send,
    ca_recv,
    q_send,
    q_recv,
    f_send,
    f_recv,
    cb_send,
    c_recv,
    fw_send,
    fd_recv,
    r_send,
    r_recv,
):
    y = lax.axis_index("req")
    s = lax.axis_index("seq")
    core = s % 2
    slot, quarter = role(s)
    sibling = s + 1 - 2 * core

    def remote(src, dst, send, recv, to):
        return pltpu.make_async_remote_copy(
            src_ref=src, dst_ref=dst, send_sem=send, recv_sem=recv, device_id=to, device_id_type=MESH
        )

    def lanes(start):
        return pl.ds(pl.multiple_of(start, 256), 256)

    def cache_part(k, h):
        return c_ref.at[:, :, lanes(h * 1024 + k * 256)]

    def stage_part(owner, h):
        return stage.at[pl.ds(2 * owner, 2), :, pl.ds(h * 256, 256)]

    for d in range(1, 4):
        k = (y + d) % 4
        for h in range(2):
            remote(
                cache_part(k, h), stage_part(y, h), ca_send.at[d, h], ca_recv.at[y, h], (k, s)
            ).start()
    for h in range(2):
        pltpu.make_async_copy(cache_part(y, h), stage_part(y, h), ca_recv.at[y, h]).start()

    def fresh_copies(k, j, p, act):
        target = device_of(2 * y + j, 2 * p + core)
        own = (k == y) & (target == s)
        n = (k * 2 + j) * 2 + p
        for h in range(2):
            src = f_ref.at[j, :, lanes(h * 1024 + k * 256)]
            dst = kvf.at[s, :, pl.ds(h * 256, 256)]

            @pl.when(jnp.logical_not(own))
            def _():
                cp = remote(src, dst, f_send.at[n, h], fd_recv.at[s, h], (k, target))
                if act == "start":
                    cp.start()
                else:
                    cp.wait_send()

            if act == "start":

                @pl.when(own)
                def _():
                    pltpu.make_async_copy(src, dst, fd_recv.at[s, h]).start()

    def query_copies(k, j, act):
        target = device_of(2 * y + j, s % 4)
        own = (k == y) & (target == s)
        n = k * 2 + j
        src = q_ref.at[j, :, pl.ds(pl.multiple_of(k * 512, 512), 512)]
        dst = qbuf.at[s // 4]

        @pl.when(jnp.logical_not(own))
        def _():
            cp = remote(src, dst, q_send.at[n], q_recv.at[s // 4], (k, target))
            if act == "start":
                cp.start()
            else:
                cp.wait_send()

        if act == "start":

            @pl.when(own)
            def _():
                pltpu.make_async_copy(src, dst, q_recv.at[s // 4]).start()

    def new_rows(act):
        for d in range(4):
            k = (y + d) % 4
            for j in range(2):
                for p in range(2):
                    fresh_copies(k, j, p, act)
        for d in range(4):
            k = (y + d) % 4
            for j in range(2):
                query_copies(k, j, act)

    new_rows("start")

    for owner in range(4):
        for h in range(2):
            pltpu.make_async_copy(stage_part(owner, h), stage_part(owner, h), ca_recv.at[owner, h]).wait()
    for i in range(8):
        order[i] = stage[slot_ref[i]]

    def cache_copies(i, p, act):
        target = device_of(i, 2 * p + core)
        own = target == s
        src = order.at[i]
        dst = kvc.at[s]

        @pl.when(jnp.logical_not(own))
        def _():
            cp = remote(src, dst, cb_send.at[i, p], c_recv.at[s], (y, target))
            if act == "start":
                cp.start()
            else:
                cp.wait_send()

        if act == "start":

            @pl.when(own)
            def _():
                pltpu.make_async_copy(src, dst, c_recv.at[s]).start()

    for i in range(8):
        for p in range(2):
            cache_copies(i, p, "start")

    for j in range(16):
        src = 2 * j + core
        for h in range(2):
            part = kvf.at[src, :, pl.ds(h * 256, 256)]
            pltpu.make_async_copy(part, part, fd_recv.at[src, h]).wait()
        remote(kvf.at[src], kvf.at[src], fw_send.at[j, 0], f_recv.at[j], (y, sibling)).start()
    for j in range(16):
        src = 2 * j + core
        pltpu.make_async_copy(kvc.at[src], kvc.at[src], c_recv.at[src]).wait()
        remote(kvc.at[src], kvc.at[src], fw_send.at[j, 1], c_recv.at[src], (y, sibling)).start()
    for j in range(8):
        pltpu.make_async_copy(qbuf.at[j], qbuf.at[j], q_recv.at[j]).wait()
    for j in range(16):
        src = 2 * j + 1 - core
        pltpu.make_async_copy(kvf.at[src], kvf.at[src], f_recv.at[j]).wait()
        pltpu.make_async_copy(kvc.at[src], kvc.at[src], c_recv.at[src]).wait()

    length = len_ref[0]
    for n in range(12):
        fresh = n - 4
        if n < 4:
            keys = kvc[8 * n : 8 * n + 8].reshape(256, 512)
            first = 0
        else:
            keys = kvf[4 * fresh : 4 * fresh + 4].reshape(256, 512)
            first = fresh
        rows = 512 - 64 * first
        for g in range(2):
            queries = qbuf[first:, :, g * 256 : (g + 1) * 256].reshape(rows, 256)
            scores = lax.dot_general(
                queries, keys[:, :256], (((1,), (1,)), ((), ())), preferred_element_type=jnp.float32
            )
            weights = jnp.exp2(
                jnp.tanh(scores * (HD**-0.5 / SOFT_CAP)) * (SOFT_CAP * LOG2E)
            )
            if 0 < n < 4:
                lane = lax.broadcasted_iota(jnp.int32, (rows, 256), 1)
                weights = jnp.where(lane + 256 * n < length, weights, 0.0)
            if n >= 4:
                lane = lax.broadcasted_iota(jnp.int32, (64, 256), 1)
                line = lax.broadcasted_iota(jnp.int32, (64, 256), 0)
                edge = jnp.where(lane <= quarter * 64 + line, weights[:64], 0.0)
                weights = jnp.concatenate([edge, weights[64:]], axis=0) if rows > 64 else edge
            rounded = weights.astype(jnp.bfloat16)
            wide = rounded.astype(jnp.float32)
            total = wide[:, :128] + wide[:, 128:]
            summed = jnp.dot(rounded, keys[:, 256:], preferred_element_type=jnp.float32)
            if n == 0:
                acc[g] = summed
                den[g] = total
            else:
                acc[g, 64 * first :, :] += summed
                den[g, 64 * first :, :] += total
    for g in range(2):
        bottom = jnp.sum(den[g], axis=-1, keepdims=True)
        obuf[:, :, g * 256 : (g + 1) * 256] = (
            (acc[g] / bottom).astype(jnp.bfloat16).reshape(8, 64, 256)
        )

    def result_copies(j, act):
        target = quarter + 4 * j
        own = target == s
        src = obuf.at[j]
        dst = att_ref.at[slot]

        @pl.when(jnp.logical_not(own))
        def _():
            cp = remote(src, dst, r_send.at[j], r_recv.at[slot], (y, target))
            if act == "start":
                cp.start()
            else:
                cp.wait_send()

        if act == "start":

            @pl.when(own)
            def _():
                pltpu.make_async_copy(src, dst, r_recv.at[slot]).start()

    for j in range(8):
        result_copies(j, "start")
    for i in range(8):
        pltpu.make_async_copy(att_ref.at[i], att_ref.at[i], r_recv.at[i]).wait()

    for d in range(1, 4):
        k = (y + d) % 4
        for h in range(2):
            remote(
                cache_part(k, h), stage_part(y, h), ca_send.at[d, h], ca_recv.at[y, h], (k, s)
            ).wait_send()
    new_rows("wait")
    for i in range(8):
        for p in range(2):
            cache_copies(i, p, "wait")
    for j in range(16):
        src = 2 * j + core
        remote(kvf.at[src], kvf.at[src], fw_send.at[j, 0], f_recv.at[j], (y, sibling)).wait_send()
        remote(kvc.at[src], kvc.at[src], fw_send.at[j, 1], c_recv.at[src], (y, sibling)).wait_send()
    for j in range(8):
        result_copies(j, "wait")


def attention(slot_request, length, query, fresh, cache):
    dma = pltpu.SemaphoreType.DMA
    return pl.pallas_call(
        attention_kernel,
        out_shape=jax.ShapeDtypeStruct((8, 64, 512), jnp.bfloat16),
        in_specs=[
            pl.BlockSpec(memory_space=pltpu.SMEM),
            pl.BlockSpec(memory_space=pltpu.SMEM),
            pl.BlockSpec(memory_space=pltpu.VMEM),
            pl.BlockSpec(memory_space=pltpu.VMEM),
            pl.BlockSpec(memory_space=pltpu.VMEM),
        ],
        out_specs=pl.BlockSpec(memory_space=pltpu.VMEM),
        scratch_shapes=[
            pltpu.VMEM((8, 64, 512), jnp.bfloat16),
            pltpu.VMEM((32, 64, 512), jnp.bfloat16),
            pltpu.VMEM((32, 32, 512), jnp.bfloat16),
            pltpu.VMEM((8, 32, 512), jnp.bfloat16),
            pltpu.VMEM((8, 32, 512), jnp.bfloat16),
            pltpu.VMEM((8, 64, 512), jnp.bfloat16),
            pltpu.VMEM((2, 512, 256), jnp.float32),
            pltpu.VMEM((2, 512, 128), jnp.float32),
            dma((4, 2)),
            dma((4, 2)),
            dma((8,)),
            dma((8,)),
            dma((16, 2)),
            dma((16,)),
            dma((8, 2)),
            dma((32,)),
            dma((16, 2)),
            dma((32, 2)),
            dma((8,)),
            dma((8,)),
        ],
        compiler_params=pltpu.CompilerParams(
            has_side_effects=True, vmem_limit_bytes=40 * 1024 * 1024
        ),
        name="attention",
    )(slot_request, length, query, fresh, cache)


def ffn_kernel(
    att_ref,
    res_ref,
    wo_hbm,
    wg_hbm,
    wu_hbm,
    wd_hbm,
    ga_ref,
    gp_ref,
    gq_ref,
    out_ref,
    wo,
    wg,
    wu,
    wd,
    parts,
    passed,
    relay,
    arrived,
    gathered,
    state,
    hidden,
    w_sem,
    rs_send,
    rs_recv,
    ag_send,
    ag_recv,
):
    y = lax.axis_index("req")
    s = lax.axis_index("seq")
    up, down = (y + 1) % 4, (y + 3) % 4
    loads = [
        pltpu.make_async_copy(src, dst, w_sem.at[n])
        for n, (src, dst) in enumerate(((wo_hbm, wo), (wg_hbm, wg), (wu_hbm, wu), (wd_hbm, wd)))
    ]
    for cp in loads:
        cp.start()
    barrier = pltpu.get_barrier_semaphore()
    for to in (up, down):
        pl.semaphore_signal(barrier, inc=1, device_id=(to, s), device_id_type=MESH)
    pl.semaphore_wait(barrier, 2)

    halves = (pl.ds(0, 32), pl.ds(32, 32))

    def remote(src, dst, send, recv, to):
        return pltpu.make_async_remote_copy(
            src_ref=src,
            dst_ref=dst,
            send_sem=send,
            recv_sem=recv,
            device_id=(to, s),
            device_id_type=MESH,
        )

    def await_copy(dst, sem):
        pltpu.make_async_copy(dst, dst, sem).wait()

    def first_copies(e, b):
        send, recv = rs_send.at[e, b], rs_recv.at[e, b]
        mine = parts.at[e, b]
        return (
            remote(mine.at[2, halves[0]], relay.at[e, b, 0], send.at[0], recv.at[0], up),
            remote(mine.at[2, halves[1]], relay.at[e, b, 1], send.at[1], recv.at[1], down),
            remote(
                mine.at[1, halves[1]], arrived.at[e, b, 0, halves[1]], send.at[2], recv.at[2], up
            ),
            remote(
                mine.at[3, halves[0]], arrived.at[e, b, 1, halves[0]], send.at[3], recv.at[3], down
            ),
        )

    def relay_copy(e, b, d):
        dst = arrived.at[e, b, d, halves[d]]
        send, recv = rs_send.at[e, b, 4 + d], rs_recv.at[e, b, 4 + d]
        return remote(passed.at[e, b, d], dst, send, recv, (up, down)[d])

    def start_sum(e, b):
        for cp in first_copies(e, b):
            cp.start()

    def relay_sum(e, b):
        for d in range(2):
            await_copy(relay.at[e, b, d], rs_recv.at[e, b, d])
            mine = parts[e, b, 1 + 2 * d, 32 * d : 32 * d + 32]
            passed[e, b, d] = (
                relay[e, b, d].astype(jnp.float32) + mine.astype(jnp.float32)
            ).astype(jnp.bfloat16)
            relay_copy(e, b, d).start()

    def finish_sum(e, b):
        await_copy(arrived.at[e, b, 0, halves[1]], rs_recv.at[e, b, 2])
        await_copy(arrived.at[e, b, 1, halves[0]], rs_recv.at[e, b, 3])
        await_copy(arrived.at[e, b, 0, halves[0]], rs_recv.at[e, b, 4])
        await_copy(arrived.at[e, b, 1, halves[1]], rs_recv.at[e, b, 5])
        return (
            parts[e, b, 0].astype(jnp.float32)
            + arrived[e, b, 0].astype(jnp.float32)
            + arrived[e, b, 1].astype(jnp.float32)
        )

    def spread_copies(b):
        send, recv = ag_send.at[b], ag_recv.at[b]
        mine = gathered.at[b, 0]
        return (
            remote(mine, gathered.at[b, 3], send.at[0], recv.at[0], up),
            remote(mine, gathered.at[b, 1], send.at[1], recv.at[1], down),
        )

    def onward_copy(b, d):
        src = gathered.at[b, 3 - 2 * d, halves[d]]
        dst = gathered.at[b, 2, halves[d]]
        send, recv = ag_send.at[b, 2 + d], ag_recv.at[b, 2 + d]
        return remote(src, dst, send, recv, (up, down)[d])

    def onward(b):
        for d in range(2):
            await_copy(gathered.at[b, 3 - 2 * d], ag_recv.at[b, d])
            onward_copy(b, d).start()

    def project(b):
        rows = jnp.concatenate([att_ref[2 * ((y + r) % 4) + b] for r in range(4)], axis=0)
        product = jnp.dot(rows, wo[...], preferred_element_type=jnp.float32)
        parts[0, b] = product.astype(jnp.bfloat16).reshape(4, 64, 2304)

    def middle(b):
        level = res_ref[b].astype(jnp.float32) + rms_scale(finish_sum(0, b), ga_ref[...])
        state[b] = level
        gathered[b, 0] = rms_scale(level, gp_ref[...]).astype(jnp.bfloat16)
        for cp in spread_copies(b):
            cp.start()

    def widen(b):
        for d in range(2):
            await_copy(gathered.at[b, 2, halves[d]], ag_recv.at[b, 2 + d])
        rows = gathered[b].reshape(256, 2304)
        gate = jnp.dot(rows, wg[...], preferred_element_type=jnp.float32)
        lift = jnp.dot(rows, wu[...], preferred_element_type=jnp.float32)
        hidden[...] = (jax.nn.gelu(gate, approximate=True) * lift).astype(jnp.bfloat16)

    def narrow(b):
        product = jnp.dot(hidden[...], wd[...], preferred_element_type=jnp.float32)
        parts[1, b] = product.astype(jnp.bfloat16).reshape(4, 64, 2304)
        start_sum(1, b)

    def last(b):
        out_ref[b] = (state[b] + rms_scale(finish_sum(1, b), gq_ref[...])).astype(jnp.bfloat16)

    loads[0].wait()
    project(0)
    start_sum(0, 0)
    project(1)
    relay_sum(0, 0)
    start_sum(0, 1)
    middle(0)
    relay_sum(0, 1)
    onward(0)
    middle(1)
    for cp in loads[1:]:
        cp.wait()
    widen(0)
    onward(1)
    narrow(0)
    widen(1)
    relay_sum(1, 0)
    narrow(1)
    last(0)
    relay_sum(1, 1)
    last(1)
    for b in range(2):
        for e in range(2):
            for cp in first_copies(e, b):
                cp.wait_send()
        for cp in spread_copies(b):
            cp.wait_send()
        for d in range(2):
            relay_copy(0, b, d).wait_send()
            relay_copy(1, b, d).wait_send()
            onward_copy(b, d).wait_send()


def feed_forward(attended, residual, w_out, w_gate, w_up, w_down, gain_attn, gain_pre, gain_post):
    dma = pltpu.SemaphoreType.DMA
    vmem = pl.BlockSpec(memory_space=pltpu.VMEM)
    hbm = pl.BlockSpec(memory_space=pl.ANY)
    bf16 = jnp.bfloat16
    return pl.pallas_call(
        ffn_kernel,
        out_shape=jax.ShapeDtypeStruct((2, 64, 2304), bf16),
        in_specs=[vmem, vmem, hbm, hbm, hbm, hbm, vmem, vmem, vmem],
        out_specs=vmem,
        scratch_shapes=[
            pltpu.VMEM(w_out.shape, bf16),
            pltpu.VMEM(w_gate.shape, bf16),
            pltpu.VMEM(w_up.shape, bf16),
            pltpu.VMEM(w_down.shape, bf16),
            pltpu.VMEM((2, 2, 4, 64, 2304), bf16),
            pltpu.VMEM((2, 2, 2, 32, 2304), bf16),
            pltpu.VMEM((2, 2, 2, 32, 2304), bf16),
            pltpu.VMEM((2, 2, 2, 64, 2304), bf16),
            pltpu.VMEM((2, 4, 64, 2304), bf16),
            pltpu.VMEM((2, 64, 2304), jnp.float32),
            pltpu.VMEM((256, 1152), bf16),
            dma((4,)),
            dma((2, 2, 6)),
            dma((2, 2, 6)),
            dma((2, 4)),
            dma((2, 4)),
        ],
        compiler_params=pltpu.CompilerParams(
            collective_id=1, has_side_effects=True, vmem_limit_bytes=52 * 1024 * 1024
        ),
        name="feed_forward",
    )(
        attended,
        residual,
        w_out,
        w_gate,
        w_up,
        w_down,
        gain_attn.reshape(1, -1),
        gain_pre.reshape(1, -1),
        gain_post.reshape(1, -1),
    )


def body(
    query,
    fresh_kv,
    residual,
    kv_cache,
    page_table,
    cache_length,
    slot_request,
    w_out,
    w_gate,
    w_up,
    w_down,
    gain_attn,
    gain_pre,
    gain_post,
):
    req_dev, row_count = (query.shape[0], query.shape[1])
    pages_dev, page_len, pair_width = kv_cache.shape[1:]
    my_seq = lax.axis_index("seq")
    ordered = jnp.where(
        (page_table[:, 0, :] == 1)[:, :, None, None], kv_cache[:, 1:2], kv_cache[:, 0:1]
    ).reshape(req_dev, pages_dev * page_len, pair_width)
    my_request = lax.dynamic_slice_in_dim(slot_request, role(my_seq)[0], 1)
    my_len = jnp.sum(
        jnp.where(my_request == jnp.arange(cache_length.shape[0]), cache_length, 0)
    ).reshape(1)
    attended = attention(slot_request, my_len, query, fresh_kv, ordered)
    return feed_forward(
        attended, residual, w_out, w_gate, w_up, w_down, gain_attn, gain_pre, gain_post
    )


def solution(mesh):
    in_specs = (
        P("req", "seq", None),
        P("req", "seq", None),
        P("req", "seq", None),
        P("req", "seq", None, None),
        P("req", "seq", None),
        P(),
        P(),
        P("req", None),
        P(None, "req"),
        P(None, "req"),
        P("req", None),
        P(),
        P(),
        P(),
    )
    out_specs = P("req", "seq", None)
    return jax.shard_map(body, mesh=mesh, in_specs=in_specs, out_specs=out_specs, check_vma=False)
```

```python
import jax
import jax.numpy as jnp
from jax import lax
from jax.experimental import pallas as pl
from jax.experimental.pallas import tpu as pltpu
from jax.sharding import PartitionSpec as P

H = 8
KV = 4
HD = 256
SOFT_CAP = 50.0
EPSILON = 1e-06
LOG2E = 1.4426950408889634
MESH = pl.DeviceIdType.MESH
VMEM_LIMIT = 67043328


def rms_scale(tensor, scale_gain):
    return (
        tensor * lax.rsqrt(jnp.mean(tensor * tensor, axis=-1, keepdims=True) + EPSILON) * scale_gain
    )


def role(s):
    x, z = s // 8, (s // 2) % 4
    return 2 * ((x + z) % 4) + x % 2, 2 * (x // 2) + s % 2


def device_of(slot, quarter):
    x = 2 * (quarter // 2) + slot % 2
    z = (slot // 2 - x + 4) % 4
    return 8 * x + 2 * z + quarter % 2


def attention_kernel(
    slot_hbm,
    len_hbm,
    page_hbm,
    q_ref,
    f_ref,
    pages_hbm,
    att_ref,
    slot_ref,
    len_ref,
    page_ref,
    pages_ref,
    c_ref,
    qbuf,
    kvf,
    kvc,
    stage,
    order,
    obuf,
    acc,
    den,
    in_sem,
    ca_send,
    ca_recv,
    q_send,
    q_recv,
    f_send,
    f_recv,
    cb_send,
    c_recv,
    fw_send,
    fd_recv,
    r_send,
    r_recv,
):
    y = lax.axis_index("req")
    s = lax.axis_index("seq")
    core = s % 2
    slot, quarter = role(s)
    sibling = s + 1 - 2 * core

    def remote(src, dst, send, recv, to):
        return pltpu.make_async_remote_copy(
            src_ref=src, dst_ref=dst, send_sem=send, recv_sem=recv, device_id=to, device_id_type=MESH
        )

    def lanes(start):
        return pl.ds(pl.multiple_of(start, 256), 256)

    loads = [
        pltpu.make_async_copy(src, dst, in_sem.at[n])
        for n, (src, dst) in enumerate(
            (
                (pages_hbm, pages_ref),
                (page_hbm, page_ref),
                (slot_hbm, slot_ref),
                (len_hbm, len_ref),
            )
        )
    ]
    for cp in loads:
        cp.start()

    barrier = pltpu.get_barrier_semaphore()

    def greet(*to):
        pl.semaphore_signal(barrier, inc=1, device_id=to, device_id_type=MESH)

    home = slot // 2
    for d in range(1, 16):
        greet(y, (s + 2 * d) % 32)
    for d in range(1, 4):
        greet((y + d) % 4, s)
    greet(y, sibling)

    @pl.when(home != y)
    def _():
        for n in range(16):
            greet(home, 2 * n + core)

    for cp in loads:
        cp.wait()
    for r in range(2):
        for j in range(2):
            c_ref[r, 16 * j : 16 * j + 16] = pages_ref[r, page_ref[r, 0, j]]

    pl.semaphore_wait(barrier, 15 + 3 + 1 + 12)

    def cache_part(k, h):
        return c_ref.at[:, :, lanes(h * 1024 + k * 256)]

    def stage_part(owner, h):
        return stage.at[pl.ds(2 * owner, 2), :, pl.ds(h * 256, 256)]

    for d in range(1, 4):
        k = (y + d) % 4
        for h in range(2):
            remote(
                cache_part(k, h), stage_part(y, h), ca_send.at[d, h], ca_recv.at[y, h], (k, s)
            ).start()
    for h in range(2):
        pltpu.make_async_copy(cache_part(y, h), stage_part(y, h), ca_recv.at[y, h]).start()

    def fresh_copies(k, j, p, act):
        target = device_of(2 * y + j, 2 * p + core)
        own = (k == y) & (target == s)
        n = (k * 2 + j) * 2 + p
        for h in range(2):
            src = f_ref.at[j, :, lanes(h * 1024 + k * 256)]
            dst = kvf.at[s, :, pl.ds(h * 256, 256)]

            @pl.when(jnp.logical_not(own))
            def _():
                cp = remote(src, dst, f_send.at[n, h], fd_recv.at[s, h], (k, target))
                if act == "start":
                    cp.start()
                else:
                    cp.wait_send()

            if act == "start":

                @pl.when(own)
                def _():
                    pltpu.make_async_copy(src, dst, fd_recv.at[s, h]).start()

    def query_copies(k, j, act):
        target = device_of(2 * y + j, s % 4)
        own = (k == y) & (target == s)
        n = k * 2 + j
        src = q_ref.at[j, :, pl.ds(pl.multiple_of(k * 512, 512), 512)]
        dst = qbuf.at[s // 4]

        @pl.when(jnp.logical_not(own))
        def _():
            cp = remote(src, dst, q_send.at[n], q_recv.at[s // 4], (k, target))
            if act == "start":
                cp.start()
            else:
                cp.wait_send()

        if act == "start":

            @pl.when(own)
            def _():
                pltpu.make_async_copy(src, dst, q_recv.at[s // 4]).start()

    def new_rows(act):
        for d in range(4):
            k = (y + d) % 4
            for j in range(2):
                for p in range(2):
                    fresh_copies(k, j, p, act)
        for d in range(4):
            k = (y + d) % 4
            for j in range(2):
                query_copies(k, j, act)

    new_rows("start")

    for owner in range(4):
        for h in range(2):
            pltpu.make_async_copy(stage_part(owner, h), stage_part(owner, h), ca_recv.at[owner, h]).wait()
    for i in range(8):
        order[i] = stage[slot_ref[i]]

    def cache_copies(i, p, act):
        target = device_of(i, 2 * p + core)
        own = target == s
        src = order.at[i]
        dst = kvc.at[s]

        @pl.when(jnp.logical_not(own))
        def _():
            cp = remote(src, dst, cb_send.at[i, p], c_recv.at[s], (y, target))
            if act == "start":
                cp.start()
            else:
                cp.wait_send()

        if act == "start":

            @pl.when(own)
            def _():
                pltpu.make_async_copy(src, dst, c_recv.at[s]).start()

    for i in range(8):
        for p in range(2):
            cache_copies(i, p, "start")

    for j in range(16):
        src = 2 * j + core
        for h in range(2):
            part = kvf.at[src, :, pl.ds(h * 256, 256)]
            pltpu.make_async_copy(part, part, fd_recv.at[src, h]).wait()
        remote(kvf.at[src], kvf.at[src], fw_send.at[j, 0], f_recv.at[j], (y, sibling)).start()
    for j in range(16):
        src = 2 * j + core
        pltpu.make_async_copy(kvc.at[src], kvc.at[src], c_recv.at[src]).wait()
        remote(kvc.at[src], kvc.at[src], fw_send.at[j, 1], c_recv.at[src], (y, sibling)).start()
    for j in range(8):
        pltpu.make_async_copy(qbuf.at[j], qbuf.at[j], q_recv.at[j]).wait()
    for j in range(16):
        src = 2 * j + 1 - core
        pltpu.make_async_copy(kvf.at[src], kvf.at[src], f_recv.at[j]).wait()
        pltpu.make_async_copy(kvc.at[src], kvc.at[src], c_recv.at[src]).wait()

    length = len_ref[slot_ref[slot]]
    for n in range(12):
        fresh = n - 4
        if n < 4:
            keys = kvc[8 * n : 8 * n + 8].reshape(256, 512)
            first = 0
        else:
            keys = kvf[4 * fresh : 4 * fresh + 4].reshape(256, 512)
            first = fresh
        rows = 512 - 64 * first
        for g in range(2):
            queries = qbuf[first:, :, g * 256 : (g + 1) * 256].reshape(rows, 256)
            scores = lax.dot_general(
                queries, keys[:, :256], (((1,), (1,)), ((), ())), preferred_element_type=jnp.float32
            )
            weights = jnp.exp2(
                jnp.tanh(scores * (HD**-0.5 / SOFT_CAP)) * (SOFT_CAP * LOG2E)
            )
            if 0 < n < 4:
                lane = lax.broadcasted_iota(jnp.int32, (rows, 256), 1)
                weights = jnp.where(lane + 256 * n < length, weights, 0.0)
            if n >= 4:
                lane = lax.broadcasted_iota(jnp.int32, (64, 256), 1)
                line = lax.broadcasted_iota(jnp.int32, (64, 256), 0)
                edge = jnp.where(lane <= quarter * 64 + line, weights[:64], 0.0)
                weights = jnp.concatenate([edge, weights[64:]], axis=0) if rows > 64 else edge
            rounded = weights.astype(jnp.bfloat16)
            wide = rounded.astype(jnp.float32)
            total = wide[:, :128] + wide[:, 128:]
            summed = jnp.dot(rounded, keys[:, 256:], preferred_element_type=jnp.float32)
            if n == 0:
                acc[g] = summed
                den[g] = total
            else:
                acc[g, 64 * first :, :] += summed
                den[g, 64 * first :, :] += total
    for g in range(2):
        bottom = jnp.sum(den[g], axis=-1, keepdims=True)
        obuf[:, :, g * 256 : (g + 1) * 256] = (
            (acc[g] / bottom).astype(jnp.bfloat16).reshape(8, 64, 256)
        )

    def result_copies(j, act):
        target = quarter + 4 * j
        own = target == s
        src = obuf.at[j]
        dst = att_ref.at[slot]

        @pl.when(jnp.logical_not(own))
        def _():
            cp = remote(src, dst, r_send.at[j], r_recv.at[slot], (y, target))
            if act == "start":
                cp.start()
            else:
                cp.wait_send()

        if act == "start":

            @pl.when(own)
            def _():
                pltpu.make_async_copy(src, dst, r_recv.at[slot]).start()

    for j in range(8):
        result_copies(j, "start")
    for i in range(8):
        pltpu.make_async_copy(att_ref.at[i], att_ref.at[i], r_recv.at[i]).wait()

    for d in range(1, 4):
        k = (y + d) % 4
        for h in range(2):
            remote(
                cache_part(k, h), stage_part(y, h), ca_send.at[d, h], ca_recv.at[y, h], (k, s)
            ).wait_send()
    new_rows("wait")
    for i in range(8):
        for p in range(2):
            cache_copies(i, p, "wait")
    for j in range(16):
        src = 2 * j + core
        remote(kvf.at[src], kvf.at[src], fw_send.at[j, 0], f_recv.at[j], (y, sibling)).wait_send()
        remote(kvc.at[src], kvc.at[src], fw_send.at[j, 1], c_recv.at[src], (y, sibling)).wait_send()
    for j in range(8):
        result_copies(j, "wait")


def attention(slot_request, cache_length, page_table, query, fresh, cache):
    dma = pltpu.SemaphoreType.DMA
    return pl.pallas_call(
        attention_kernel,
        out_shape=jax.ShapeDtypeStruct((8, 64, 512), jnp.bfloat16),
        in_specs=[pl.BlockSpec(memory_space=pltpu.HBM)] * 6,
        out_specs=pl.BlockSpec(memory_space=pltpu.VMEM),
        scratch_shapes=[
            pltpu.SMEM((8,), jnp.int32),
            pltpu.SMEM((8,), jnp.int32),
            pltpu.SMEM((2, 1, 2), jnp.int32),
            pltpu.VMEM((2, 2, 16, 2048), jnp.bfloat16),
            pltpu.VMEM((2, 32, 2048), jnp.bfloat16),
            pltpu.VMEM((8, 64, 512), jnp.bfloat16),
            pltpu.VMEM((32, 64, 512), jnp.bfloat16),
            pltpu.VMEM((32, 32, 512), jnp.bfloat16),
            pltpu.VMEM((8, 32, 512), jnp.bfloat16),
            pltpu.VMEM((8, 32, 512), jnp.bfloat16),
            pltpu.VMEM((8, 64, 512), jnp.bfloat16),
            pltpu.VMEM((2, 512, 256), jnp.float32),
            pltpu.VMEM((2, 512, 128), jnp.float32),
            dma((4,)),
            dma((4, 2)),
            dma((4, 2)),
            dma((8,)),
            dma((8,)),
            dma((16, 2)),
            dma((16,)),
            dma((8, 2)),
            dma((32,)),
            dma((16, 2)),
            dma((32, 2)),
            dma((8,)),
            dma((8,)),
        ],
        compiler_params=pltpu.CompilerParams(
            collective_id=0, has_side_effects=True, vmem_limit_bytes=VMEM_LIMIT
        ),
        name="attention",
    )(slot_request, cache_length, page_table, query, fresh, cache)


def ffn_kernel(
    att_ref,
    res_hbm,
    wo_hbm,
    wg_hbm,
    wu_hbm,
    wd_hbm,
    ga_hbm,
    gp_hbm,
    gq_hbm,
    out_ref,
    ga_ref,
    gp_ref,
    gq_ref,
    res_ref,
    wo,
    wg,
    wu,
    wd,
    parts,
    passed,
    relay,
    arrived,
    gathered,
    state,
    hidden,
    w_sem,
    rs_send,
    rs_recv,
    ag_send,
    ag_recv,
):
    y = lax.axis_index("req")
    s = lax.axis_index("seq")
    up, down = (y + 1) % 4, (y + 3) % 4
    loads = [
        pltpu.make_async_copy(src, dst, w_sem.at[n])
        for n, (src, dst) in enumerate(
            (
                (wo_hbm, wo),
                (res_hbm, res_ref),
                (ga_hbm, ga_ref),
                (gp_hbm, gp_ref),
                (gq_hbm, gq_ref),
                (wg_hbm, wg),
                (wu_hbm, wu),
                (wd_hbm, wd),
            )
        )
    ]
    for cp in loads:
        cp.start()
    barrier = pltpu.get_barrier_semaphore()
    for to in (up, down):
        pl.semaphore_signal(barrier, inc=1, device_id=(to, s), device_id_type=MESH)
    pl.semaphore_wait(barrier, 2)

    halves = (pl.ds(0, 32), pl.ds(32, 32))

    def remote(src, dst, send, recv, to):
        return pltpu.make_async_remote_copy(
            src_ref=src,
            dst_ref=dst,
            send_sem=send,
            recv_sem=recv,
            device_id=(to, s),
            device_id_type=MESH,
        )

    def await_copy(dst, sem):
        pltpu.make_async_copy(dst, dst, sem).wait()

    def first_copies(e, b):
        send, recv = rs_send.at[e, b], rs_recv.at[e, b]
        mine = parts.at[e, b]
        return (
            remote(mine.at[2, halves[0]], relay.at[e, b, 0], send.at[0], recv.at[0], up),
            remote(mine.at[2, halves[1]], relay.at[e, b, 1], send.at[1], recv.at[1], down),
            remote(
                mine.at[1, halves[1]], arrived.at[e, b, 0, halves[1]], send.at[2], recv.at[2], up
            ),
            remote(
                mine.at[3, halves[0]], arrived.at[e, b, 1, halves[0]], send.at[3], recv.at[3], down
            ),
        )

    def relay_copy(e, b, d):
        dst = arrived.at[e, b, d, halves[d]]
        send, recv = rs_send.at[e, b, 4 + d], rs_recv.at[e, b, 4 + d]
        return remote(passed.at[e, b, d], dst, send, recv, (up, down)[d])

    def start_sum(e, b):
        for cp in first_copies(e, b):
            cp.start()

    def relay_sum(e, b):
        for d in range(2):
            await_copy(relay.at[e, b, d], rs_recv.at[e, b, d])
            mine = parts[e, b, 1 + 2 * d, 32 * d : 32 * d + 32]
            passed[e, b, d] = (
                relay[e, b, d].astype(jnp.float32) + mine.astype(jnp.float32)
            ).astype(jnp.bfloat16)
            relay_copy(e, b, d).start()

    def finish_sum(e, b):
        await_copy(arrived.at[e, b, 0, halves[1]], rs_recv.at[e, b, 2])
        await_copy(arrived.at[e, b, 1, halves[0]], rs_recv.at[e, b, 3])
        await_copy(arrived.at[e, b, 0, halves[0]], rs_recv.at[e, b, 4])
        await_copy(arrived.at[e, b, 1, halves[1]], rs_recv.at[e, b, 5])
        return (
            parts[e, b, 0].astype(jnp.float32)
            + arrived[e, b, 0].astype(jnp.float32)
            + arrived[e, b, 1].astype(jnp.float32)
        )

    def spread_copies(b):
        send, recv = ag_send.at[b], ag_recv.at[b]
        mine = gathered.at[b, 0]
        return (
            remote(mine, gathered.at[b, 3], send.at[0], recv.at[0], up),
            remote(mine, gathered.at[b, 1], send.at[1], recv.at[1], down),
        )

    def onward_copy(b, d):
        src = gathered.at[b, 3 - 2 * d, halves[d]]
        dst = gathered.at[b, 2, halves[d]]
        send, recv = ag_send.at[b, 2 + d], ag_recv.at[b, 2 + d]
        return remote(src, dst, send, recv, (up, down)[d])

    def onward(b):
        for d in range(2):
            await_copy(gathered.at[b, 3 - 2 * d], ag_recv.at[b, d])
            onward_copy(b, d).start()

    def project(b):
        rows = jnp.concatenate([att_ref[2 * ((y + r) % 4) + b] for r in range(4)], axis=0)
        product = jnp.dot(rows, wo[...], preferred_element_type=jnp.float32)
        parts[0, b] = product.astype(jnp.bfloat16).reshape(4, 64, 2304)

    def middle(b):
        level = res_ref[b].astype(jnp.float32) + rms_scale(finish_sum(0, b), ga_ref[...][None, :])
        state[b] = level
        gathered[b, 0] = rms_scale(level, gp_ref[...][None, :]).astype(jnp.bfloat16)
        for cp in spread_copies(b):
            cp.start()

    def widen(b):
        for d in range(2):
            await_copy(gathered.at[b, 2, halves[d]], ag_recv.at[b, 2 + d])
        rows = gathered[b].reshape(256, 2304)
        gate = jnp.dot(rows, wg[...], preferred_element_type=jnp.float32)
        lift = jnp.dot(rows, wu[...], preferred_element_type=jnp.float32)
        hidden[...] = (jax.nn.gelu(gate, approximate=True) * lift).astype(jnp.bfloat16)

    def narrow(b):
        product = jnp.dot(hidden[...], wd[...], preferred_element_type=jnp.float32)
        parts[1, b] = product.astype(jnp.bfloat16).reshape(4, 64, 2304)
        start_sum(1, b)

    def last(b):
        out_ref[b] = (state[b] + rms_scale(finish_sum(1, b), gq_ref[...][None, :])).astype(jnp.bfloat16)

    loads[0].wait()
    project(0)
    start_sum(0, 0)
    project(1)
    relay_sum(0, 0)
    start_sum(0, 1)
    for cp in loads[1:5]:
        cp.wait()
    middle(0)
    relay_sum(0, 1)
    onward(0)
    middle(1)
    for cp in loads[5:]:
        cp.wait()
    widen(0)
    onward(1)
    narrow(0)
    widen(1)
    relay_sum(1, 0)
    narrow(1)
    last(0)
    relay_sum(1, 1)
    last(1)
    for b in range(2):
        for e in range(2):
            for cp in first_copies(e, b):
                cp.wait_send()
        for cp in spread_copies(b):
            cp.wait_send()
        for d in range(2):
            relay_copy(0, b, d).wait_send()
            relay_copy(1, b, d).wait_send()
            onward_copy(b, d).wait_send()


def feed_forward(attended, residual, w_out, w_gate, w_up, w_down, gain_attn, gain_pre, gain_post):
    dma = pltpu.SemaphoreType.DMA
    vmem = pl.BlockSpec(memory_space=pltpu.VMEM)
    hbm = pl.BlockSpec(memory_space=pltpu.HBM)
    bf16 = jnp.bfloat16
    return pl.pallas_call(
        ffn_kernel,
        out_shape=jax.ShapeDtypeStruct((2, 64, 2304), bf16),
        in_specs=[vmem] + [hbm] * 8,
        out_specs=vmem,
        scratch_shapes=[
            pltpu.VMEM(gain_attn.shape, jnp.float32),
            pltpu.VMEM(gain_attn.shape, jnp.float32),
            pltpu.VMEM(gain_attn.shape, jnp.float32),
            pltpu.VMEM(residual.shape, bf16),
            pltpu.VMEM(w_out.shape, bf16),
            pltpu.VMEM(w_gate.shape, bf16),
            pltpu.VMEM(w_up.shape, bf16),
            pltpu.VMEM(w_down.shape, bf16),
            pltpu.VMEM((2, 2, 4, 64, 2304), bf16),
            pltpu.VMEM((2, 2, 2, 32, 2304), bf16),
            pltpu.VMEM((2, 2, 2, 32, 2304), bf16),
            pltpu.VMEM((2, 2, 2, 64, 2304), bf16),
            pltpu.VMEM((2, 4, 64, 2304), bf16),
            pltpu.VMEM((2, 64, 2304), jnp.float32),
            pltpu.VMEM((256, 1152), bf16),
            dma((8,)),
            dma((2, 2, 6)),
            dma((2, 2, 6)),
            dma((2, 4)),
            dma((2, 4)),
        ],
        compiler_params=pltpu.CompilerParams(
            collective_id=1, has_side_effects=True, vmem_limit_bytes=VMEM_LIMIT
        ),
        name="feed_forward",
    )(
        attended,
        residual,
        w_out,
        w_gate,
        w_up,
        w_down,
        gain_attn,
        gain_pre,
        gain_post,
    )


def body(
    query,
    fresh_kv,
    residual,
    kv_cache,
    page_table,
    cache_length,
    slot_request,
    w_out,
    w_gate,
    w_up,
    w_down,
    gain_attn,
    gain_pre,
    gain_post,
):
    attended = attention(
        slot_request, cache_length, page_table, query, fresh_kv, kv_cache
    )
    return feed_forward(
        attended, residual, w_out, w_gate, w_up, w_down, gain_attn, gain_pre, gain_post
    )


def solution(mesh):
    in_specs = (
        P("req", "seq", None),
        P("req", "seq", None),
        P("req", "seq", None),
        P("req", "seq", None, None),
        P("req", "seq", None),
        P(),
        P(),
        P("req", None),
        P(None, "req"),
        P(None, "req"),
        P("req", None),
        P(),
        P(),
        P(),
    )
    out_specs = P("req", "seq", None)
    return jax.shard_map(body, mesh=mesh, in_specs=in_specs, out_specs=out_specs, check_vma=False)
```
